512 devices in a mesh: ctx: 64 (over y, z_hi, core), fsdp: 8 (over z_lo, x).
Axes of the slice: x: 4, y: 8, z: 8 (z_hi: 4, z_lo: 2; z = z_hi * 2 + z_lo), core: 2. Of those that a mesh axis runs over, the one named last changes fastest.
Arguments:
- query_act: bfloat16 [16384, 3072], P('ctx', 'fsdp'), may hold values from -10 to 10
- key_act: bfloat16 [16384, 3072], P('ctx', 'fsdp'), may hold values from -4 to 4
- value_act: bfloat16 [16384, 3072], P('ctx', 'fsdp'), may hold values from -6 to 6
- resid_in: bfloat16 [16384, 3072], P('ctx', 'fsdp'), may hold values from -60 to 60
- gate_vec: float32 [3072], P('fsdp'), may hold values from 0.5 to 2.5
- mod_scale: float32 [3072], P('fsdp'), may hold values from -2.5 to 2.5
- mod_shift: float32 [3072], P('fsdp'), may hold values from -3 to 3
- w_up: bfloat16 [3072, 6912], P(('ctx', 'fsdp')), may hold values from -0.109375 to 0.109375
- bias_up: float32 [6912], P('fsdp'), may hold values from -3 to 3
Outputs:
- residual: bfloat16 [16384, 3072], P('ctx', 'fsdp')
- hidden: bfloat16 [16384, 6912], P('ctx', 'fsdp')
The draws below stay inside these ranges and needn't reach their ends.
All inputs are finite; a program needn't handle non-finite values.
Results may differ from the reference program's by a relative error of at most 0.0059.
Values may be sent and summed in bfloat16 or wider, within the bound.
A program may use at most 64 MiB of HBM per device.

```python
import math
import jax
import jax.numpy as jnp
from jax import lax

HEADS = 24
HEAD = 128
FFW = 6912
TOK_DEV = 256
D = 3072
WIN = 128
SEQ = 16384


def draw_query_act(key, part):
    noise_key = jax.random.fold_in(key, 7)
    sampled = 2.0 * jax.random.truncated_normal(noise_key, -5.0, 5.0, (SEQ, D), jnp.float32)
    return sampled.astype(jnp.bfloat16)


def draw_key_act(key, part):
    noise_key = jax.random.fold_in(key, 9)
    sampled = jax.random.truncated_normal(noise_key, -4.0, 4.0, (SEQ, D), jnp.float32)
    return sampled.astype(jnp.bfloat16)


def draw_resid_in(key, part):
    row_key = jax.random.fold_in(key, 21)
    col_key = jax.random.fold_in(key, 22)
    noise_key = jax.random.fold_in(key, 23)
    row_scale = jnp.exp(jax.random.uniform(row_key, (SEQ, 1), jnp.float32, math.log(0.3), math.log(3.0)))
    frac = jnp.arange(D, dtype=jnp.float32)[None, :] / D
    jitter = jnp.exp(jax.random.uniform(col_key, (1, D), jnp.float32, math.log(0.8), math.log(1.25)))
    col_scale = 0.3 * jnp.exp(math.log(10.0) * frac) * jitter
    sampled = row_scale * col_scale * jax.random.truncated_normal(noise_key, -3.0, 3.0, (SEQ, D), jnp.float32)
    return sampled.astype(jnp.bfloat16)


def block_scale(rng, shape, pieces, smallest, high):
    gain = 1.0
    for position, blocks in pieces:
        draws = jax.random.uniform(jax.random.fold_in(jax.random.fold_in(rng, 6), position), (blocks,), jnp.float32, smallest / len(pieces), high / len(pieces))
        gain = gain * jnp.repeat(jnp.exp(draws), shape[position] // blocks).reshape((-1,) + (1,) * (len(shape) - 1 - position))
    return gain


def bell_draw(rng, extent, scale, most, shards=(), kind=jnp.bfloat16):
    drawn = scale * jax.random.normal(rng, extent, jnp.float32)
    if shards:
        drawn = drawn * block_scale(rng, extent, shards, -0.22, 0.18)
    return jnp.clip(drawn, -most, most).astype(kind)


def setup_inputs(seed: int = 0) -> dict:
    key_list = jax.random.split(jax.random.key(seed), 10)
    query_act = draw_query_act(jax.random.fold_in(key_list[9], 71), 0)
    key_act = draw_key_act(jax.random.fold_in(key_list[9], 71), 0)
    value_act = bell_draw(key_list[2], (SEQ, D), 1.0, 6.0, ((0, 64), (1, 8)))
    resid_in = draw_resid_in(jax.random.fold_in(key_list[9], 71), 0)
    gate_vec = jnp.clip(0.5 + 2.0 * jax.random.uniform(key_list[4], (D,), jnp.float32) ** block_scale(key_list[4], (D,), ((0, 8),), -0.2, 0.2), 0.5, 2.5)
    mod_scale = bell_draw(key_list[5], (D,), 0.3, 2.5, ((0, 8),), jnp.float32)
    mod_shift = bell_draw(key_list[6], (D,), 0.5, 3.0, ((0, 8),), jnp.float32)
    w_up = bell_draw(key_list[7], (D, FFW), D ** -0.5, 0.109375, ((0, 512),))
    bias_up = bell_draw(key_list[8], (FFW,), 0.5, 3.0, ((0, 8),), jnp.float32)
    return dict(query_act=query_act, key_act=key_act, value_act=value_act, resid_in=resid_in, gate_vec=gate_vec, mod_scale=mod_scale, mod_shift=mod_shift, w_up=w_up, bias_up=bias_up)


def reference(query_act, key_act, value_act, resid_in, gate_vec, mod_scale, mod_shift, w_up, bias_up):
    blocks = SEQ // TOK_DEV
    zero_pad = jnp.zeros((WIN, D), jnp.bfloat16)
    key_pad = jnp.concatenate([zero_pad, key_act, zero_pad], axis=0)
    value_pad = jnp.concatenate([zero_pad, value_act, zero_pad], axis=0)
    scale_qk = 1.0 / math.sqrt(HEAD)

    def one_block(block_idx):
        row_start = (block_idx * TOK_DEV).astype(jnp.int32)
        query_blk = lax.dynamic_slice_in_dim(query_act, row_start, TOK_DEV, 0)
        key_blk = lax.dynamic_slice_in_dim(key_pad, row_start, TOK_DEV + 2 * WIN, 0)
        value_blk = lax.dynamic_slice_in_dim(value_pad, row_start, TOK_DEV + 2 * WIN, 0)
        resid_blk = lax.dynamic_slice_in_dim(resid_in, row_start, TOK_DEV, 0)
        query_pos = row_start + jnp.arange(TOK_DEV, dtype=jnp.int32)
        key_pos = row_start - WIN + jnp.arange(TOK_DEV + 2 * WIN, dtype=jnp.int32)
        allowed = (jnp.abs(query_pos[:, None] - key_pos[None, :]) <= WIN) & (key_pos[None, :] >= 0) & (key_pos[None, :] < SEQ)
        query_heads = query_blk.reshape(TOK_DEV, HEADS, HEAD).astype(jnp.float32)
        key_heads = key_blk.reshape(TOK_DEV + 2 * WIN, HEADS, HEAD).astype(jnp.float32)
        value_heads = value_blk.reshape(TOK_DEV + 2 * WIN, HEADS, HEAD).astype(jnp.float32)
        scores = jnp.einsum('qhd,khd->hqk', query_heads, key_heads) * scale_qk
        masked = jnp.where(allowed[None], scores, -jnp.inf)
        row_max = lax.optimization_barrier(jnp.max(masked, axis=2, keepdims=True))
        exp_terms = jnp.exp(masked - row_max)
        attn_probs = (exp_terms / lax.optimization_barrier(jnp.sum(exp_terms, axis=2, keepdims=True))).astype(jnp.bfloat16)
        attended = jnp.einsum('hqk,khd->qhd', attn_probs.astype(jnp.float32), value_heads)
        attended = attended.reshape(TOK_DEV, D).astype(jnp.bfloat16)
        residual_out = (resid_blk.astype(jnp.float32) + gate_vec * attended.astype(jnp.float32)).astype(jnp.bfloat16)
        rows_float = residual_out.astype(jnp.float32)
        mean_val = lax.optimization_barrier(jnp.mean(rows_float, axis=1, keepdims=True))
        centered = rows_float - mean_val
        var_val = lax.optimization_barrier(jnp.mean(centered * centered, axis=1, keepdims=True))
        normed = (centered * lax.rsqrt(var_val + 1e-06) * (1.0 + mod_scale) + mod_shift).astype(jnp.bfloat16)
        pre_act = jnp.dot(normed, w_up, preferred_element_type=jnp.float32) + bias_up
        hidden_blk = jax.nn.gelu(pre_act, approximate=True).astype(jnp.bfloat16)
        return (residual_out, hidden_blk)
    residual_all, hidden_all = lax.map(one_block, jnp.arange(blocks, dtype=jnp.int32))
    return (residual_all.reshape(SEQ, D), hidden_all.reshape(SEQ, FFW))
```

```python
import functools
import math

import jax
import jax.numpy as jnp
from jax import lax
from jax.experimental import pallas as pl
from jax.experimental.pallas import tpu as pltpu
from jax.sharding import PartitionSpec as P

HEAD = 128
NY, NZ, NC = 8, 4, 2

MESH = pl.DeviceIdType.MESH
F32, BF16 = jnp.float32, jnp.bfloat16


def kernel(
    count_f,
    q_hbm,
    k_hbm,
    v_hbm,
    r_hbm,
    gate_hbm,
    scale_hbm,
    shift_hbm,
    w_hbm,
    bias_hbm,
    res_hbm,
    hid_hbm,
    q_buf,
    kv_buf,
    r_buf,
    vec_in,
    w_buf,
    bias_buf,
    w_send,
    w_recv,
    w_pack,
    wall,
    xg,
    xn,
    vecs,
    acc,
    hid_buf,
    local_sem,
    send_sem,
    recv_sem,
):
    tok, feat = q_buf.shape
    reach = tok // 2
    rows = w_buf.shape[0]
    wide = bias_buf.shape[1]
    d_model = feat * count_f
    me = lax.axis_index("ctx")
    f = lax.axis_index("fsdp")
    count_c = NY * NZ * NC
    y = lax.div(me, NZ * NC)
    zh = lax.rem(lax.div(me, NC), NZ)
    core = lax.rem(me, NC)

    def ctx_of(yy, zz, cc):
        return (yy * NZ + zz) * NC + cc

    right = (ctx_of(lax.rem(y + 1, NY), zh, core), f)
    left = (ctx_of(lax.rem(y + NY - 1, NY), zh, core), f)
    sibling = (ctx_of(y, zh, 1 - core), f)
    before = (lax.rem(me + count_c - 1, count_c), f)
    after = (lax.rem(me + 1, count_c), f)
    f_peers = [(me, lax.rem(f + d, count_f)) for d in range(1, count_f)]
    z_peers = [(ctx_of(y, lax.rem(zh + d, NZ), core), f) for d in range(1, NZ)]

    partners = [right, left, sibling, before, after] + f_peers + z_peers
    barrier = pltpu.get_barrier_semaphore()
    for dev in partners:
        pl.semaphore_signal(barrier, inc=1, device_id=dev, device_id_type=MESH)

    used = [0]
    loads = []

    def load(src, dst):
        copy = pltpu.make_async_copy(src, dst, local_sem.at[len(loads)])
        copy.start()
        loads.append(copy)
        return copy

    started = []

    def send(src, dst, dev):
        n = used[0]
        used[0] += 1
        copy = pltpu.make_async_remote_copy(
            src_ref=src,
            dst_ref=dst,
            send_sem=send_sem.at[n],
            recv_sem=recv_sem.at[n],
            device_id=dev,
            device_id_type=MESH,
        )
        copy.start()
        started.append(copy)
        return copy

    load_w = load(w_hbm, w_buf)
    load_vec = [
        load(scale_hbm, vec_in.at[0]),
        load(shift_hbm, vec_in.at[1]),
        load(gate_hbm, vec_in.at[2]),
        load(bias_hbm, bias_buf),
    ]
    load_k = load(k_hbm, kv_buf.at[0, pl.ds(reach, tok)])
    load_v = load(v_hbm, kv_buf.at[1, pl.ds(reach, tok)])
    load_q = load(q_hbm, q_buf)
    load_r = load(r_hbm, r_buf)

    load_w.wait()
    w_rows = w_buf[...].astype(F32)
    for g in range(count_f):
        w_send[g, 0:rows, 0:wide] = w_rows[:, g * wide : (g + 1) * wide]
    for copy in load_vec:
        copy.wait()
    vecs[f, 0:1, :] = 1.0 + vec_in[0]
    vecs[f, 1:2, :] = vec_in[1]

    pl.semaphore_wait(barrier, len(partners))

    cols_in = [send(w_send.at[dev[1]], w_recv.at[f], dev) for dev in f_peers]
    halo_in = []
    for i, src in enumerate((k_hbm, v_hbm)):
        halo_in.append(send(src.at[pl.ds(tok - reach, reach)], kv_buf.at[i, pl.ds(0, reach)], after))
        halo_in.append(
            send(src.at[pl.ds(0, reach)], kv_buf.at[i, pl.ds(reach + tok, reach)], before)
        )
    vecs_in = [send(vecs.at[f], vecs.at[f], dev) for dev in f_peers]

    w_recv[f] = w_send[f]
    for copy in cols_in:
        copy.wait_recv()
    for g in range(count_f):
        w_pack[rows * g : rows * (g + 1), :] = w_recv[g, 0:rows, :]
    wall[y, zh, core] = w_pack[...].astype(BF16)
    z_in = [send(wall.at[y, zh, core], wall.at[y, zh, core], dev) for dev in z_peers]

    first_pos = me * tok
    seq_total = tok * count_c
    scale_qk = 1.0 / math.sqrt(HEAD)

    def attend(block):
        start = block * reach
        shape = (reach, 3 * reach)
        row_id = lax.broadcasted_iota(jnp.int32, shape, 0)
        col_id = lax.broadcasted_iota(jnp.int32, shape, 1)
        key_pos = first_pos + (start - reach) + col_id
        offset = col_id - row_id
        allowed = (
            (offset >= 0) & (offset <= 2 * reach) & (key_pos >= 0) & (key_pos < seq_total)
        )
        for h in range(feat // HEAD):
            cols = slice(h * HEAD, (h + 1) * HEAD)
            qs = q_buf[start : start + reach, cols]
            ks = kv_buf[0, start : start + 3 * reach, cols]
            vs = kv_buf[1, start : start + 3 * reach, cols]
            scores = (
                lax.dot_general(qs, ks, (((1,), (1,)), ((), ())), preferred_element_type=F32)
                * scale_qk
            )
            masked = jnp.where(allowed, scores, -jnp.inf)
            row_max = jnp.max(masked, axis=1, keepdims=True)
            terms = jnp.exp(masked - row_max)
            probs = (terms / jnp.sum(terms, axis=1, keepdims=True)).astype(BF16)
            attended = jnp.dot(probs, vs, preferred_element_type=F32).astype(BF16)
            resid = r_buf[start : start + reach, cols].astype(F32)
            gate = vec_in[2, :, cols]
            xg[f, start : start + reach, cols] = (resid + gate * attended.astype(F32)).astype(BF16)
        part = pl.ds(start, reach)
        return [send(xg.at[f, part], xg.at[f, part], dev) for dev in f_peers]

    for copy in (load_k, load_v, load_q, load_r):
        copy.wait()
    for copy in halo_in:
        copy.wait_recv()
    x_in = [attend(0)]

    for copy in z_in:
        copy.wait_recv()

    half = NZ // 2
    reach_y = NY // 2

    def hop(source, part, dev):
        ref = wall.at[source, pl.ds(part * half, half), core]
        return send(ref, ref, dev)

    def share(source):
        ref = wall.at[source, :, core]
        return send(ref, ref, sibling)

    def at(shift):
        return lax.rem(y + shift + NY, NY)

    ring = {}
    for part in range(2):
        ring["r", part] = hop(y, part, right)
        ring["l", 1 - part] = hop(y, 1 - part, left)
    shared = {0: share(y)}

    x_in.append(attend(1))
    store_res = pltpu.make_async_copy(xg.at[f], res_hbm, local_sem.at[len(loads)])
    store_res.start()

    for copy in vecs_in:
        copy.wait_recv()

    def normalise(block):
        for copy in x_in[block]:
            copy.wait_recv()
        part = slice(block * reach, (block + 1) * reach)
        total = jnp.zeros((reach, feat), F32)
        for g in range(count_f):
            total += xg[g, part, :].astype(F32)
        mean = jnp.sum(total, axis=1, keepdims=True) / d_model
        total = jnp.zeros((reach, feat), F32)
        for g in range(count_f):
            centered = xg[g, part, :].astype(F32) - mean
            total += centered * centered
        inv = lax.rsqrt(jnp.sum(total, axis=1, keepdims=True) / d_model + 1e-06)
        for g in range(count_f):
            centered = xg[g, part, :].astype(F32) - mean
            xn[g, part, :] = (centered * inv * vecs[g, 0:1, :] + vecs[g, 1:2, :]).astype(BF16)

    def multiply(shift, first=False):
        shared[shift].wait_recv()
        source = at(shift)
        weights = wall[source].reshape(NZ * NC * rows * count_f, wall.shape[-1])
        part = jnp.dot(xn[source], weights, preferred_element_type=F32)
        if first:
            acc[...] = part
        else:
            acc[...] += part

    for step in range(1, reach_y):
        for part in range(2):
            for way, dev, sign in (("r", right, -1), ("l", left, 1)):
                piece = part if way == "r" else 1 - part
                ring[way, piece].wait_recv()
                if step + 1 < reach_y or piece == (0 if way == "r" else 1):
                    ring[way, piece] = hop(at(sign * step), piece, dev)
        shared[-step] = share(at(-step))
        shared[step] = share(at(step))
        if step == 1:
            normalise(0)
        elif step == 2:
            normalise(1)
            multiply(0, first=True)
        else:
            multiply(-1)
            multiply(1)
    multiply(-2)
    multiply(2)
    ring["r", 0].wait_recv()
    ring["l", 1].wait_recv()
    shared[reach_y] = share(at(reach_y))
    multiply(-3)
    multiply(3)
    multiply(reach_y)

    pre = acc[:, 0:wide] + bias_buf[...]
    hid_buf[...] = jax.nn.gelu(pre, approximate=True).astype(BF16)
    store_hid = pltpu.make_async_copy(hid_buf, hid_hbm, local_sem.at[len(loads) + 1])
    store_hid.start()
    for copy in started:
        copy.wait_send()
    store_res.wait()
    store_hid.wait()


def shards(query_act, key_act, value_act, resid_in, gate_vec, mod_scale, mod_shift, w_up, bias_up):
    tok, feat = query_act.shape
    count_f = lax.axis_size("fsdp")
    wide = bias_up.shape[0]
    padded = -(-wide // 128) * 128
    rows = w_up.shape[0]
    row_pad = -(-rows // 8) * 8
    sends = 4 * (count_f - 1) + 4 + (NZ - 1) + 2 * (NY - 1) + NY
    anywhere = pl.BlockSpec(memory_space=pl.ANY)
    return pl.pallas_call(
        functools.partial(kernel, count_f),
        out_shape=(
            jax.ShapeDtypeStruct((tok, feat), BF16),
            jax.ShapeDtypeStruct((tok, wide), BF16),
        ),
        in_specs=[anywhere] * 9,
        out_specs=(anywhere, anywhere),
        scratch_shapes=[
            pltpu.VMEM((tok, feat), BF16),
            pltpu.VMEM((2, 2 * tok, feat), BF16),
            pltpu.VMEM((tok, feat), BF16),
            pltpu.VMEM((3, 1, feat), F32),
            pltpu.VMEM((rows, w_up.shape[1]), BF16),
            pltpu.VMEM((1, wide), F32),
            pltpu.VMEM((count_f, row_pad, padded), F32),
            pltpu.VMEM((count_f, row_pad, padded), F32),
            pltpu.VMEM((rows * count_f, padded), F32),
            pltpu.VMEM((NY, NZ, NC, rows * count_f, padded), BF16),
            pltpu.VMEM((count_f, tok, feat), BF16),
            pltpu.VMEM((count_f, tok, feat), BF16),
            pltpu.VMEM((count_f, 8, feat), F32),
            pltpu.VMEM((tok, padded), F32),
            pltpu.VMEM((tok, wide), BF16),
            pltpu.SemaphoreType.DMA((11,)),
            pltpu.SemaphoreType.DMA((sends,)),
            pltpu.SemaphoreType.DMA((sends,)),
        ],
        compiler_params=pltpu.CompilerParams(
            collective_id=0, has_side_effects=True, vmem_limit_bytes=48 * 1024 * 1024
        ),
    )(
        query_act,
        key_act,
        value_act,
        resid_in,
        gate_vec.reshape(1, feat),
        mod_scale.reshape(1, feat),
        mod_shift.reshape(1, feat),
        w_up,
        bias_up.reshape(1, wide),
    )


def solution(mesh):
    placed = (
        P("ctx", "fsdp"),
        P("ctx", "fsdp"),
        P("ctx", "fsdp"),
        P("ctx", "fsdp"),
        P("fsdp"),
        P("fsdp"),
        P("fsdp"),
        P(("ctx", "fsdp"), None),
        P("fsdp"),
    )
    return jax.shard_map(
        shards,
        mesh=mesh,
        in_specs=placed,
        out_specs=(P("ctx", "fsdp"), P("ctx", "fsdp")),
        check_vma=False,
    )
```

```python
import functools
import math

import jax
import jax.numpy as jnp
from jax import lax
from jax.experimental import pallas as pl
from jax.experimental.pallas import tpu as pltpu
from jax.sharding import PartitionSpec as P

HEAD = 128
NY, NZ, NC = 8, 4, 2
NX = 4

MESH = pl.DeviceIdType.MESH
F32, BF16 = jnp.float32, jnp.bfloat16


def kernel(
    count_f,
    q_hbm,
    k_hbm,
    v_hbm,
    r_hbm,
    gate_hbm,
    scale_hbm,
    shift_hbm,
    w_hbm,
    bias_hbm,
    res_hbm,
    hid_hbm,
    q_buf,
    kv_buf,
    r_buf,
    scale_buf,
    shift_buf,
    gate_buf,
    w_buf,
    bias_buf,
    w_send,
    w_recv,
    w_pack,
    wall,
    xg,
    xn,
    vecs,
    acc,
    hid_buf,
    local_sem,
    send_sem,
    recv_sem,
    ready_sem,
):
    tok, feat = q_buf.shape
    reach = tok // 2
    rows = w_buf.shape[0]
    wide = bias_buf.shape[0]
    d_model = feat * count_f
    me = lax.axis_index("ctx")
    f = lax.axis_index("fsdp")
    count_c = NY * NZ * NC
    y = lax.div(me, NZ * NC)
    zh = lax.rem(lax.div(me, NC), NZ)
    core = lax.rem(me, NC)
    odd = lax.rem(zh, 2)
    zs = (zh, zh + 1 - 2 * odd, lax.rem(zh + 2, NZ), NZ - 1 - zh)
    late = lax.div(zh, 2)

    def ctx_of(yy, zz, cc):
        return (yy * NZ + zz) * NC + cc

    right = (ctx_of(lax.rem(y + 1, NY), zh, core), f)
    left = (ctx_of(lax.rem(y + NY - 1, NY), zh, core), f)
    sibling = (ctx_of(y, zh, 1 - core), f)
    f_peers = [(me, lax.rem(f + d, count_f)) for d in range(1, count_f)]
    row = lax.div(f, NX) * NX
    x_peers = [(me, row + lax.rem(f + d, NX)) for d in (1, 3, 2)]
    beside = lax.rem(f + NX, count_f)
    z_peers = [None] + [(ctx_of(y, zs[j], core), f) for j in range(1, NZ)]
    far = (lax.rem(me + 2 * core - 1 + count_c, count_c), f)
    crossing = 1 - lax.rem(odd + core, 2)

    barrier = pltpu.get_barrier_semaphore()
    near = [right, left, sibling, z_peers[1]] + f_peers

    def greet(dev):
        pl.semaphore_signal(barrier, inc=1, device_id=dev, device_id_type=MESH)

    for dev in near:
        greet(dev)

    @pl.when(late == 0)
    def _():
        greet(z_peers[3])

    @pl.when(late * crossing == 0)
    def _():
        greet(far)

    used = [0]
    loads = []

    def load(src, dst):
        copy = pltpu.make_async_copy(src, dst, local_sem.at[len(loads)])
        copy.start()
        loads.append(copy)
        return copy

    started = []

    def prepare(src, dst, dev):
        n = used[0]
        used[0] += 1
        copy = pltpu.make_async_remote_copy(
            src_ref=src,
            dst_ref=dst,
            send_sem=send_sem.at[n],
            recv_sem=recv_sem.at[n],
            device_id=dev,
            device_id_type=MESH,
        )
        started.append(copy)
        return copy

    def send(src, dst, dev):
        copy = prepare(src, dst, dev)
        copy.start()
        return copy

    load_w = load(w_hbm, w_buf)
    load_k = load(k_hbm, kv_buf.at[0, pl.ds(reach, tok)])
    load_v = load(v_hbm, kv_buf.at[1, pl.ds(reach, tok)])
    load_q = load(q_hbm, q_buf)
    load_r = load(r_hbm, r_buf)
    load_vec = [
        load(scale_hbm, scale_buf),
        load(shift_hbm, shift_buf),
        load(gate_hbm, gate_buf),
        load(bias_hbm, bias_buf),
    ]

    load_w.wait()
    w_rows = w_buf[...].astype(F32)
    for g in range(count_f):
        w_send[g, 0:rows, 0:wide] = w_rows[:, g * wide : (g + 1) * wide].astype(BF16)
    for copy in [load_k, load_v, load_q, load_r] + load_vec:
        copy.wait()
    vecs[f, 0:1, :] = 1.0 + scale_buf[...].reshape(1, feat)
    vecs[f, 1:2, :] = shift_buf[...].reshape(1, feat)

    pl.semaphore_wait(barrier, len(near) + (1 - crossing) + late * (1 + crossing))

    cols_in = [send(w_send.at[dev[1]], w_recv.at[f], dev) for dev in f_peers]
    own_edge = pl.multiple_of(reach + (1 - core) * reach, reach)
    far_edge = pl.multiple_of(reach + core * reach, reach)
    low_halo, high_halo = 0, reach + tok
    near_slot = pl.multiple_of((1 - core) * low_halo + core * high_halo, reach)
    far_slot = pl.multiple_of((1 - core) * high_halo + core * low_halo, reach)
    near_halo = send(kv_buf.at[:, pl.ds(own_edge, reach)], kv_buf.at[:, pl.ds(near_slot, reach)], sibling)
    far_halo = prepare(kv_buf.at[:, pl.ds(far_edge, reach)], kv_buf.at[:, pl.ds(far_slot, reach)], far)

    @pl.when(late == 1)
    def _():
        pl.semaphore_signal(ready_sem.at[0], inc=1, device_id=z_peers[3], device_id_type=MESH)

    @pl.when(late * crossing == 1)
    def _():
        pl.semaphore_signal(ready_sem.at[1], inc=1, device_id=far, device_id_type=MESH)

    asks = (1 - late) * crossing

    @pl.when(asks == 0)
    def _():
        far_halo.start()

    w_recv[f] = w_send[f]
    for copy in cols_in:
        copy.wait_recv()
    for g in range(count_f):
        w_pack[rows * g : rows * (g + 1), :] = w_recv[g, 0:rows, :].astype(F32)
    wall[y, zh, core] = w_pack[...].astype(BF16)
    mine = wall.at[y, zh, core]

    ring = {}
    reach_y = NY // 2
    hops = {0: (reach_y, reach_y - 1), 1: (reach_y - 1, reach_y)}

    def at(shift):
        return lax.rem(y + shift + NY, NY)

    def pass_on(j, hop):
        for way, dev, sign in ((0, right, -1), (1, left, 1)):
            last = hops[j % 2][way]
            if 1 <= hop <= last:
                ring[j, way].wait_recv()
            if hop < last:
                ref = wall.at[at(sign * hop), zs[j], core]
                ring[j, way] = send(ref, ref, dev)

    def half_of(j):
        return lax.div(zs[j], 2)

    shared = {}

    def share(j, shift):
        ref = wall.at[at(shift), pl.ds(2 * half_of(j), 2), core]
        shared[j, shift] = send(ref, ref, sibling)

    pass_on(0, 0)
    z_in = [None, send(mine, mine, z_peers[1])]
    z_in += [None, prepare(mine, mine, z_peers[3])]

    @pl.when(late == 1)
    def _():
        z_in[3].start()

    vecs_in = [send(vecs.at[f], vecs.at[f], dev) for dev in f_peers]

    first_pos = me * tok
    seq_total = tok * count_c
    scale_qk = 1.0 / math.sqrt(HEAD)

    def attend(block):
        start = pl.multiple_of(block * reach, reach)
        part = pl.ds(start, reach)
        shape = (reach, 3 * reach)
        row_id = lax.broadcasted_iota(jnp.int32, shape, 0)
        col_id = lax.broadcasted_iota(jnp.int32, shape, 1)
        key_pos = first_pos + (start - reach) + col_id
        offset = col_id - row_id
        allowed = (
            (offset >= 0) & (offset <= 2 * reach) & (key_pos >= 0) & (key_pos < seq_total)
        )
        for h in range(feat // HEAD):
            cols = slice(h * HEAD, (h + 1) * HEAD)
            qs = q_buf[part, cols]
            ks = kv_buf[0, pl.ds(start, 3 * reach), cols]
            vs = kv_buf[1, pl.ds(start, 3 * reach), cols]
            scores = (
                lax.dot_general(qs, ks, (((1,), (1,)), ((), ())), preferred_element_type=F32)
                * scale_qk
            )
            masked = jnp.where(allowed, scores, -jnp.inf)
            row_max = jnp.max(masked, axis=1, keepdims=True)
            terms = jnp.exp(masked - row_max)
            probs = (terms / jnp.sum(terms, axis=1, keepdims=True)).astype(BF16)
            attended = jnp.dot(probs, vs, preferred_element_type=F32).astype(BF16)
            resid = r_buf[part, cols].astype(F32)
            gate = gate_buf[cols].reshape(1, HEAD)
            xg[f, part, cols] = (resid + gate * attended.astype(F32)).astype(BF16)
        mine = xg.at[f, part]
        return [send(mine, mine, dev) for dev in [(me, beside)] + x_peers]

    def part_of(order):
        return pl.ds(pl.multiple_of(((1 - core) if order == 0 else core) * reach, reach), reach)

    def relay(order):
        x_in[order].pop(0).wait_recv()
        theirs = xg.at[beside, part_of(order)]
        x_in[order] += [send(theirs, theirs, dev) for dev in x_peers]

    def normalise(order):
        for copy in x_in[order]:
            copy.wait_recv()
        part = part_of(order)
        total = jnp.zeros((reach, feat), F32)
        for g in range(count_f):
            total += xg[g, part, :].astype(F32)
        mean = jnp.sum(total, axis=1, keepdims=True) / d_model
        total = jnp.zeros((reach, feat), F32)
        for g in range(count_f):
            centered = xg[g, part, :].astype(F32) - mean
            total += centered * centered
        inv = lax.rsqrt(jnp.sum(total, axis=1, keepdims=True) / d_model + 1e-06)
        for g in range(count_f):
            centered = xg[g, part, :].astype(F32) - mean
            xn[g, part, :] = (centered * inv * vecs[g, 0:1, :] + vecs[g, 1:2, :]).astype(BF16)

    def multiply(shift, first=False):
        shared[1, shift].wait_recv()
        shared[3, shift].wait_recv()
        source = at(shift)
        weights = wall[source].reshape(NZ * NC * rows * count_f, wall.shape[-1])
        part = jnp.dot(xn[source], weights, preferred_element_type=F32)
        if first:
            acc[...] = part
        else:
            acc[...] += part

    near_halo.wait_recv()
    x_in = [attend(1 - core)]
    pass_on(0, 1)

    @pl.when(late == 0)
    def _():
        pl.semaphore_wait(ready_sem.at[0], 1)
        z_in[3].start()

    @pl.when(asks == 1)
    def _():
        pl.semaphore_wait(ready_sem.at[1], 1)
        far_halo.start()

    z_in[1].wait_recv()
    pass_on(1, 0)
    relay(0)
    share(1, 0)
    pass_on(0, 2)
    pass_on(1, 1)
    far_halo.wait_recv()
    x_in.append(attend(core))
    store_res = pltpu.make_async_copy(xg.at[f], res_hbm, local_sem.at[len(loads)])
    store_res.start()
    pass_on(0, 3)
    share(1, -1)
    share(1, 1)
    z_in[3].wait_recv()
    theirs = wall.at[y, zs[3], core]
    z_in[2] = send(theirs, theirs, z_peers[1])
    pass_on(3, 0)
    pass_on(1, 2)
    share(1, -2)
    share(1, 2)
    relay(1)
    z_in[2].wait_recv()
    pass_on(2, 0)
    share(3, 0)
    pass_on(0, 4)
    pass_on(1, 3)
    share(1, -3)
    share(1, 3)
    pass_on(3, 1)
    for copy in vecs_in:
        copy.wait_recv()
    normalise(0)
    pass_on(2, 1)
    share(3, -1)
    share(3, 1)
    pass_on(1, 4)
    share(1, reach_y)
    pass_on(3, 2)
    pass_on(2, 2)
    share(3, -2)
    share(3, 2)
    normalise(1)
    multiply(0, first=True)
    pass_on(3, 3)
    pass_on(2, 3)
    share(3, -3)
    share(3, 3)
    multiply(-1)
    multiply(1)
    multiply(-2)
    multiply(2)
    pass_on(3, 4)
    pass_on(2, 4)
    share(3, reach_y)
    multiply(-3)
    multiply(3)
    multiply(reach_y)

    pre = acc[:, 0:wide] + bias_buf[...].reshape(1, wide)
    hid_buf[...] = jax.nn.gelu(pre, approximate=True).astype(BF16)
    store_hid = pltpu.make_async_copy(hid_buf, hid_hbm, local_sem.at[len(loads) + 1])
    store_hid.start()
    for copy in started:
        copy.wait_send()
    store_res.wait()
    store_hid.wait()


def shards(query_act, key_act, value_act, resid_in, gate_vec, mod_scale, mod_shift, w_up, bias_up):
    tok, feat = query_act.shape
    count_f = lax.axis_size("fsdp")
    wide = bias_up.shape[0]
    padded = -(-wide // 128) * 128
    rows = w_up.shape[0]
    row_pad = -(-rows // 8) * 8
    sends = 4 * (count_f - 1) + 2 + (NZ - 1) + NZ * (NY - 1) + 2 * NY
    anywhere = pl.BlockSpec(memory_space=pl.ANY)
    return pl.pallas_call(
        functools.partial(kernel, count_f),
        out_shape=(
            jax.ShapeDtypeStruct((tok, feat), BF16),
            jax.ShapeDtypeStruct((tok, wide), BF16),
        ),
        in_specs=[anywhere] * 9,
        out_specs=(anywhere, anywhere),
        scratch_shapes=[
            pltpu.VMEM((tok, feat), BF16),
            pltpu.VMEM((2, 2 * tok, feat), BF16),
            pltpu.VMEM((tok, feat), BF16),
            pltpu.VMEM((feat,), F32),
            pltpu.VMEM((feat,), F32),
            pltpu.VMEM((feat,), F32),
            pltpu.VMEM((rows, w_up.shape[1]), BF16),
            pltpu.VMEM((wide,), F32),
            pltpu.VMEM((count_f, row_pad, padded), BF16),
            pltpu.VMEM((count_f, row_pad, padded), BF16),
            pltpu.VMEM((rows * count_f, padded), F32),
            pltpu.VMEM((NY, NZ, NC, rows * count_f, padded), BF16),
            pltpu.VMEM((count_f, tok, feat), BF16),
            pltpu.VMEM((count_f, tok, feat), BF16),
            pltpu.VMEM((count_f, 2, feat), F32),
            pltpu.VMEM((tok, padded), F32),
            pltpu.VMEM((tok, wide), BF16),
            pltpu.SemaphoreType.DMA((11,)),
            pltpu.SemaphoreType.DMA((sends,)),
            pltpu.SemaphoreType.DMA((sends,)),
            pltpu.SemaphoreType.REGULAR((2,)),
        ],
        compiler_params=pltpu.CompilerParams(
            collective_id=0, has_side_effects=True, vmem_limit_bytes=60 * 1024 * 1024
        ),
    )(
        query_act,
        key_act,
        value_act,
        resid_in,
        gate_vec,
        mod_scale,
        mod_shift,
        w_up,
        bias_up,
    )


def solution(mesh):
    placed = (
        P("ctx", "fsdp"),
        P("ctx", "fsdp"),
        P("ctx", "fsdp"),
        P("ctx", "fsdp"),
        P("fsdp"),
        P("fsdp"),
        P("fsdp"),
        P(("ctx", "fsdp"), None),
        P("fsdp"),
    )
    return jax.shard_map(
        shards,
        mesh=mesh,
        in_specs=placed,
        out_specs=(P("ctx", "fsdp"), P("ctx", "fsdp")),
        check_vma=False,
    )
```

```python
import functools
import math

import jax
import jax.numpy as jnp
from jax import lax
from jax.experimental import pallas as pl
from jax.experimental.pallas import tpu as pltpu
from jax.sharding import PartitionSpec as P

HEAD = 128
NY, NZ, NC = 8, 4, 2
NX = 4

MESH = pl.DeviceIdType.MESH
F32, BF16 = jnp.float32, jnp.bfloat16


def kernel(
    count_f,
    q_hbm,
    k_hbm,
    v_hbm,
    r_hbm,
    gate_hbm,
    scale_hbm,
    shift_hbm,
    w_hbm,
    bias_hbm,
    res_hbm,
    hid_hbm,
    q_buf,
    kv_buf,
    r_buf,
    scale_buf,
    shift_buf,
    gate_buf,
    w_buf,
    bias_buf,
    w_send,
    w_recv,
    w_pack,
    wall,
    xg,
    xn,
    vecs,
    acc,
    hid_buf,
    local_sem,
    send_sem,
    recv_sem,
    ready_sem,
):
    tok, feat = q_buf.shape
    reach = tok // 2
    rows = w_buf.shape[0]
    wide = bias_buf.shape[0]
    d_model = feat * count_f
    me = lax.axis_index("ctx")
    f = lax.axis_index("fsdp")
    count_c = NY * NZ * NC
    y = lax.div(me, NZ * NC)
    zh = lax.rem(lax.div(me, NC), NZ)
    core = lax.rem(me, NC)
    odd = lax.rem(zh, 2)
    zs = (zh, zh + 1 - 2 * odd, lax.rem(zh + 2, NZ), NZ - 1 - zh)
    late = lax.div(zh, 2)

    def ctx_of(yy, zz, cc):
        return (yy * NZ + zz) * NC + cc

    right = (ctx_of(lax.rem(y + 1, NY), zh, core), f)
    left = (ctx_of(lax.rem(y + NY - 1, NY), zh, core), f)
    sibling = (ctx_of(y, zh, 1 - core), f)
    f_peers = [(me, lax.rem(f + d, count_f)) for d in range(1, count_f)]
    row = lax.div(f, NX) * NX
    x_peers = [(me, row + lax.rem(f + d, NX)) for d in (1, 3, 2)]
    beside = lax.rem(f + NX, count_f)
    z_peers = [None] + [(ctx_of(y, zs[j], core), f) for j in range(1, NZ)]
    far = (lax.rem(me + 2 * core - 1 + count_c, count_c), f)
    crossing = 1 - lax.rem(odd + core, 2)

    barrier = pltpu.get_barrier_semaphore()
    near = [right, left, sibling, z_peers[1]] + f_peers

    def greet(dev):
        pl.semaphore_signal(barrier, inc=1, device_id=dev, device_id_type=MESH)

    for dev in near:
        greet(dev)

    @pl.when(late == 0)
    def _():
        greet(z_peers[3])

    @pl.when(late * crossing == 0)
    def _():
        greet(far)

    used = [0]
    loads = []

    def load(src, dst):
        copy = pltpu.make_async_copy(src, dst, local_sem.at[len(loads)])
        copy.start()
        loads.append(copy)
        return copy

    started = []

    def prepare(src, dst, dev):
        n = used[0]
        used[0] += 1
        copy = pltpu.make_async_remote_copy(
            src_ref=src,
            dst_ref=dst,
            send_sem=send_sem.at[n],
            recv_sem=recv_sem.at[n],
            device_id=dev,
            device_id_type=MESH,
        )
        started.append(copy)
        return copy

    def send(src, dst, dev):
        copy = prepare(src, dst, dev)
        copy.start()
        return copy

    load_w = load(w_hbm, w_buf)
    load_k = load(k_hbm, kv_buf.at[0, pl.ds(reach, tok)])
    load_v = load(v_hbm, kv_buf.at[1, pl.ds(reach, tok)])
    load_q = load(q_hbm, q_buf)
    load_r = load(r_hbm, r_buf)
    load_vec = [
        load(scale_hbm, scale_buf),
        load(shift_hbm, shift_buf),
        load(gate_hbm, gate_buf),
        load(bias_hbm, bias_buf),
    ]

    load_w.wait()
    w_rows = w_buf[...].astype(F32)
    for g in range(count_f):
        w_send[g, 0:rows, 0:wide] = w_rows[:, g * wide : (g + 1) * wide].astype(BF16)
    for copy in [load_k, load_v, load_q, load_r] + load_vec:
        copy.wait()
    vecs[f, 0:1, :] = 1.0 + scale_buf[...].reshape(1, feat)
    vecs[f, 1:2, :] = shift_buf[...].reshape(1, feat)

    pl.semaphore_wait(barrier, len(near) + (1 - crossing) + late * (1 + crossing))

    cols_in = [send(w_send.at[dev[1]], w_recv.at[f], dev) for dev in f_peers]
    own_edge = pl.multiple_of(reach + (1 - core) * reach, reach)
    far_edge = pl.multiple_of(reach + core * reach, reach)
    low_halo, high_halo = 0, reach + tok
    near_slot = pl.multiple_of((1 - core) * low_halo + core * high_halo, reach)
    far_slot = pl.multiple_of((1 - core) * high_halo + core * low_halo, reach)
    near_halo = send(kv_buf.at[:, pl.ds(own_edge, reach)], kv_buf.at[:, pl.ds(near_slot, reach)], sibling)
    far_halo = prepare(kv_buf.at[:, pl.ds(far_edge, reach)], kv_buf.at[:, pl.ds(far_slot, reach)], far)

    @pl.when(late == 1)
    def _():
        pl.semaphore_signal(ready_sem.at[0], inc=1, device_id=z_peers[3], device_id_type=MESH)

    @pl.when(late * crossing == 1)
    def _():
        pl.semaphore_signal(ready_sem.at[1], inc=1, device_id=far, device_id_type=MESH)

    asks = (1 - late) * crossing

    w_recv[f] = w_send[f]
    for copy in cols_in:
        copy.wait_recv()
    for g in range(count_f):
        w_pack[rows * g : rows * (g + 1), :] = w_recv[g, 0:rows, :].astype(F32)
    wall[y, zh, core] = w_pack[...].astype(BF16)

    ring = {}
    reach_y = NY // 2
    hops = ((reach_y, reach_y - 1), (reach_y - 1, reach_y))
    tiles = wall.shape[-1] // 128
    cut = (tiles + 1) // 2 * 128
    lanes = (pl.ds(0, cut), pl.ds(cut, tiles * 128 - cut))

    def at(shift):
        return lax.rem(y + shift + NY, NY)

    def piece(source, j, p):
        return wall.at[source, zs[j], core, :, lanes[p]]

    def pass_on(j, hop, p=None):
        if p is None:
            for p in range(len(hops)):
                pass_on(j, hop, p)
            return
        for way, dev, sign in ((0, right, -1), (1, left, 1)):
            last = hops[p][way]
            if 1 <= hop <= last:
                ring[j, p, way].wait_recv()
            if hop < last:
                ref = piece(at(sign * hop), j, p)
                ring[j, p, way] = send(ref, ref, dev)

    def half_of(j):
        return lax.div(zs[j], 2)

    shared = {}

    def share(j, shift):
        ref = wall.at[at(shift), pl.ds(2 * half_of(j), 2), core]
        shared[j, shift] = send(ref, ref, sibling)

    pass_on(0, 0)
    z_in = {}
    for p in range(len(hops)):
        z_in[1, p] = send(piece(y, 0, p), piece(y, 0, p), z_peers[1])
    for p in range(len(hops)):
        z_in[3, p] = prepare(piece(y, 0, p), piece(y, 0, p), z_peers[3])

    @pl.when(late == 1)
    def _():
        for p in range(len(hops)):
            z_in[3, p].start()


    first_pos = me * tok
    seq_total = tok * count_c
    scale_qk = 1.0 / math.sqrt(HEAD)

    def attend(block):
        start = pl.multiple_of(block * reach, reach)
        part = pl.ds(start, reach)
        shape = (reach, 3 * reach)
        row_id = lax.broadcasted_iota(jnp.int32, shape, 0)
        col_id = lax.broadcasted_iota(jnp.int32, shape, 1)
        key_pos = first_pos + (start - reach) + col_id
        offset = col_id - row_id
        allowed = (
            (offset >= 0) & (offset <= 2 * reach) & (key_pos >= 0) & (key_pos < seq_total)
        )
        for h in range(feat // HEAD):
            cols = slice(h * HEAD, (h + 1) * HEAD)
            qs = q_buf[part, cols]
            ks = kv_buf[0, pl.ds(start, 3 * reach), cols]
            vs = kv_buf[1, pl.ds(start, 3 * reach), cols]
            scores = (
                lax.dot_general(qs, ks, (((1,), (1,)), ((), ())), preferred_element_type=F32)
                * scale_qk
            )
            masked = jnp.where(allowed, scores, -jnp.inf)
            row_max = jnp.max(masked, axis=1, keepdims=True)
            terms = jnp.exp(masked - row_max)
            probs = (terms / jnp.sum(terms, axis=1, keepdims=True)).astype(BF16)
            attended = jnp.dot(probs, vs, preferred_element_type=F32).astype(BF16)
            resid = r_buf[part, cols].astype(F32)
            gate = gate_buf[cols].reshape(1, HEAD)
            xg[f, part, cols] = (resid + gate * attended.astype(F32)).astype(BF16)
        mine = xg.at[f, part]
        return [send(mine, mine, dev) for dev in [(me, beside)] + x_peers]

    def part_of(order):
        return pl.ds(pl.multiple_of(((1 - core) if order == 0 else core) * reach, reach), reach)

    def relay(order):
        x_in[order].pop(0).wait_recv()
        theirs = xg.at[beside, part_of(order)]
        x_in[order] += [send(theirs, theirs, dev) for dev in x_peers]

    def normalise(order):
        for copy in x_in[order]:
            copy.wait_recv()
        part = part_of(order)
        total = jnp.zeros((reach, feat), F32)
        for g in range(count_f):
            total += xg[g, part, :].astype(F32)
        mean = jnp.sum(total, axis=1, keepdims=True) / d_model
        total = jnp.zeros((reach, feat), F32)
        for g in range(count_f):
            centered = xg[g, part, :].astype(F32) - mean
            total += centered * centered
        inv = lax.rsqrt(jnp.sum(total, axis=1, keepdims=True) / d_model + 1e-06)
        for g in range(count_f):
            centered = xg[g, part, :].astype(F32) - mean
            xn[g, part, :] = (centered * inv * vecs[g, 0:1, :] + vecs[g, 1:2, :]).astype(BF16)

    def multiply(shift, first=False):
        shared[1, shift].wait_recv()
        shared[3, shift].wait_recv()
        source = at(shift)
        weights = wall[source].reshape(NZ * NC * rows * count_f, wall.shape[-1])
        part = jnp.dot(xn[source], weights, preferred_element_type=F32)
        if first:
            acc[...] = part
        else:
            acc[...] += part

    near_halo.wait_recv()
    x_in = [attend(1 - core)]
    pass_on(0, 1)

    @pl.when(asks == 0)
    def _():
        far_halo.start()

    @pl.when(late == 0)
    def _():
        pl.semaphore_wait(ready_sem.at[0], 1)
        for p in range(len(hops)):
            z_in[3, p].start()

    @pl.when(asks == 1)
    def _():
        pl.semaphore_wait(ready_sem.at[1], 1)
        far_halo.start()

    for p in range(len(hops)):
        z_in[1, p].wait_recv()
        pass_on(1, 0, p)
    pass_on(0, 2)
    relay(0)
    vecs_in = [send(vecs.at[f], vecs.at[f], dev) for dev in f_peers]
    share(1, 0)
    pass_on(1, 1)
    for p in range(len(hops)):
        z_in[3, p].wait_recv()
        z_in[2, p] = send(piece(y, 3, p), piece(y, 3, p), z_peers[1])
        pass_on(3, 0, p)
    pass_on(0, 3)
    far_halo.wait_recv()
    x_in.append(attend(core))
    store_res = pltpu.make_async_copy(xg.at[f], res_hbm, local_sem.at[len(loads)])
    store_res.start()
    share(1, -1)
    share(1, 1)
    pass_on(1, 2)
    share(1, -2)
    share(1, 2)
    for p in range(len(hops)):
        z_in[2, p].wait_recv()
        pass_on(2, 0, p)
    share(3, 0)
    pass_on(0, 4)
    pass_on(3, 1)
    relay(1)
    pass_on(1, 3)
    share(1, -3)
    share(1, 3)
    pass_on(2, 1)
    share(3, -1)
    share(3, 1)
    pass_on(1, 4)
    share(1, reach_y)
    pass_on(3, 2)
    for copy in vecs_in:
        copy.wait_recv()
    normalise(0)
    pass_on(2, 2)
    share(3, -2)
    share(3, 2)
    pass_on(3, 3)
    pass_on(2, 3)
    share(3, -3)
    share(3, 3)
    normalise(1)
    multiply(0, first=True)
    multiply(-1)
    multiply(1)
    multiply(-2)
    multiply(2)
    multiply(-3)
    multiply(3)
    pass_on(3, 4)
    pass_on(2, 4)
    share(3, reach_y)
    multiply(reach_y)

    pre = acc[:, 0:wide] + bias_buf[...].reshape(1, wide)
    hid_buf[...] = jax.nn.gelu(pre, approximate=True).astype(BF16)
    store_hid = pltpu.make_async_copy(hid_buf, hid_hbm, local_sem.at[len(loads) + 1])
    store_hid.start()
    for copy in started:
        copy.wait_send()
    store_res.wait()
    store_hid.wait()


def shards(query_act, key_act, value_act, resid_in, gate_vec, mod_scale, mod_shift, w_up, bias_up):
    tok, feat = query_act.shape
    count_f = lax.axis_size("fsdp")
    wide = bias_up.shape[0]
    padded = -(-wide // 128) * 128
    rows = w_up.shape[0]
    row_pad = -(-rows // 8) * 8
    sends = 4 * (count_f - 1) + 2 + 2 * (NZ - 1) + 2 * NZ * (NY - 1) + 2 * NY
    anywhere = pl.BlockSpec(memory_space=pl.ANY)
    return pl.pallas_call(
        functools.partial(kernel, count_f),
        out_shape=(
            jax.ShapeDtypeStruct((tok, feat), BF16),
            jax.ShapeDtypeStruct((tok, wide), BF16),
        ),
        in_specs=[anywhere] * 9,
        out_specs=(anywhere, anywhere),
        scratch_shapes=[
            pltpu.VMEM((tok, feat), BF16),
            pltpu.VMEM((2, 2 * tok, feat), BF16),
            pltpu.VMEM((tok, feat), BF16),
            pltpu.VMEM((feat,), F32),
            pltpu.VMEM((feat,), F32),
            pltpu.VMEM((feat,), F32),
            pltpu.VMEM((rows, w_up.shape[1]), BF16),
            pltpu.VMEM((wide,), F32),
            pltpu.VMEM((count_f, row_pad, padded), BF16),
            pltpu.VMEM((count_f, row_pad, padded), BF16),
            pltpu.VMEM((rows * count_f, padded), F32),
            pltpu.VMEM((NY, NZ, NC, rows * count_f, padded), BF16),
            pltpu.VMEM((count_f, tok, feat), BF16),
            pltpu.VMEM((count_f, tok, feat), BF16),
            pltpu.VMEM((count_f, 2, feat), F32),
            pltpu.VMEM((tok, padded), F32),
            pltpu.VMEM((tok, wide), BF16),
            pltpu.SemaphoreType.DMA((11,)),
            pltpu.SemaphoreType.DMA((sends,)),
            pltpu.SemaphoreType.DMA((sends,)),
            pltpu.SemaphoreType.REGULAR((2,)),
        ],
        compiler_params=pltpu.CompilerParams(
            collective_id=0, has_side_effects=True, vmem_limit_bytes=48 * 1024 * 1024
        ),
    )(
        pltpu.with_memory_space_constraint(query_act, pltpu.HBM),
        pltpu.with_memory_space_constraint(key_act, pltpu.HBM),
        pltpu.with_memory_space_constraint(value_act, pltpu.HBM),
        pltpu.with_memory_space_constraint(resid_in, pltpu.HBM),
        pltpu.with_memory_space_constraint(gate_vec, pltpu.HBM),
        pltpu.with_memory_space_constraint(mod_scale, pltpu.HBM),
        pltpu.with_memory_space_constraint(mod_shift, pltpu.HBM),
        pltpu.with_memory_space_constraint(w_up, pltpu.HBM),
        pltpu.with_memory_space_constraint(bias_up, pltpu.HBM),
    )


def solution(mesh):
    placed = (
        P("ctx", "fsdp"),
        P("ctx", "fsdp"),
        P("ctx", "fsdp"),
        P("ctx", "fsdp"),
        P("fsdp"),
        P("fsdp"),
        P("fsdp"),
        P(("ctx", "fsdp"), None),
        P("fsdp"),
    )
    return jax.shard_map(
        shards,
        mesh=mesh,
        in_specs=placed,
        out_specs=(P("ctx", "fsdp"), P("ctx", "fsdp")),
        check_vma=False,
    )
```

```python
import functools
import math

import jax
import jax.numpy as jnp
from jax import lax
from jax.experimental import pallas as pl
from jax.experimental.pallas import tpu as pltpu
from jax.sharding import PartitionSpec as P

HEAD = 128
NY, NZ, NC = 8, 4, 2
NX = 4

MESH = pl.DeviceIdType.MESH
F32, BF16 = jnp.float32, jnp.bfloat16


def kernel(
    count_f,
    q_hbm,
    k_hbm,
    v_hbm,
    r_hbm,
    gate_hbm,
    scale_hbm,
    shift_hbm,
    w_hbm,
    bias_hbm,
    res_hbm,
    hid_hbm,
    q_buf,
    kv_buf,
    r_buf,
    scale_buf,
    shift_buf,
    gate_buf,
    w_buf,
    bias_buf,
    w_send,
    w_recv,
    w_pack,
    wall,
    xg,
    xn,
    vecs,
    acc,
    hid_buf,
    local_sem,
    send_sem,
    recv_sem,
    ready_sem,
):
    tok, feat = q_buf.shape
    reach = tok // 2
    rows = w_buf.shape[0]
    wide = bias_buf.shape[0]
    d_model = feat * count_f
    me = lax.axis_index("ctx")
    f = lax.axis_index("fsdp")
    count_c = NY * NZ * NC
    y = lax.div(me, NZ * NC)
    zh = lax.rem(lax.div(me, NC), NZ)
    core = lax.rem(me, NC)
    odd = lax.rem(zh, 2)
    zs = (zh, zh + 1 - 2 * odd, lax.rem(zh + 2, NZ), NZ - 1 - zh)
    late = lax.div(zh, 2)

    def ctx_of(yy, zz, cc):
        return (yy * NZ + zz) * NC + cc

    right = (ctx_of(lax.rem(y + 1, NY), zh, core), f)
    left = (ctx_of(lax.rem(y + NY - 1, NY), zh, core), f)
    sibling = (ctx_of(y, zh, 1 - core), f)
    f_peers = [(me, lax.rem(f + d, count_f)) for d in range(1, count_f)]
    row = lax.div(f, NX) * NX
    x_peers = [(me, row + lax.rem(f + d, NX)) for d in (1, 3, 2)]
    beside = lax.rem(f + NX, count_f)
    z_peers = [None] + [(ctx_of(y, zs[j], core), f) for j in range(1, NZ)]
    far = (lax.rem(me + 2 * core - 1 + count_c, count_c), f)
    crossing = 1 - lax.rem(odd + core, 2)

    barrier = pltpu.get_barrier_semaphore()
    near = [right, left, sibling, z_peers[1]] + f_peers

    def greet(dev):
        pl.semaphore_signal(barrier, inc=1, device_id=dev, device_id_type=MESH)

    for dev in near:
        greet(dev)

    @pl.when(late == 0)
    def _():
        greet(z_peers[3])

    @pl.when(late * crossing == 0)
    def _():
        greet(far)

    used = [0]
    loads = []

    def load(src, dst):
        copy = pltpu.make_async_copy(src, dst, local_sem.at[len(loads)])
        copy.start()
        loads.append(copy)
        return copy

    started = []

    def prepare(src, dst, dev):
        n = used[0]
        used[0] += 1
        copy = pltpu.make_async_remote_copy(
            src_ref=src,
            dst_ref=dst,
            send_sem=send_sem.at[n],
            recv_sem=recv_sem.at[n],
            device_id=dev,
            device_id_type=MESH,
        )
        started.append(copy)
        return copy

    def send(src, dst, dev):
        copy = prepare(src, dst, dev)
        copy.start()
        return copy

    load_w = load(w_hbm, w_buf)
    load_k = load(k_hbm, kv_buf.at[0, pl.ds(reach, tok)])
    load_v = load(v_hbm, kv_buf.at[1, pl.ds(reach, tok)])
    load_q = load(q_hbm, q_buf)
    load_r = load(r_hbm, r_buf)
    load_vec = [
        load(scale_hbm, scale_buf),
        load(shift_hbm, shift_buf),
        load(gate_hbm, gate_buf),
        load(bias_hbm, bias_buf),
    ]

    load_w.wait()
    w_rows = w_buf[...].astype(F32)
    for g in range(count_f):
        w_send[g, 0:rows, 0:wide] = w_rows[:, g * wide : (g + 1) * wide].astype(BF16)
    for copy in [load_k, load_v, load_q, load_r] + load_vec:
        copy.wait()
    vecs[f, 0:1, :] = 1.0 + scale_buf[...].reshape(1, feat)
    vecs[f, 1:2, :] = shift_buf[...].reshape(1, feat)

    pl.semaphore_wait(barrier, len(near) + (1 - crossing) + late * (1 + crossing))

    cols_in = [send(w_send.at[dev[1]], w_recv.at[f], dev) for dev in f_peers]
    own_edge = pl.multiple_of(reach + (1 - core) * reach, reach)
    far_edge = pl.multiple_of(reach + core * reach, reach)
    low_halo, high_halo = 0, reach + tok
    near_slot = pl.multiple_of((1 - core) * low_halo + core * high_halo, reach)
    far_slot = pl.multiple_of((1 - core) * high_halo + core * low_halo, reach)
    near_halo = send(kv_buf.at[:, pl.ds(own_edge, reach)], kv_buf.at[:, pl.ds(near_slot, reach)], sibling)
    far_halo = prepare(kv_buf.at[:, pl.ds(far_edge, reach)], kv_buf.at[:, pl.ds(far_slot, reach)], far)

    @pl.when(late == 1)
    def _():
        pl.semaphore_signal(ready_sem.at[0], inc=1, device_id=z_peers[3], device_id_type=MESH)

    @pl.when(late * crossing == 1)
    def _():
        pl.semaphore_signal(ready_sem.at[1], inc=1, device_id=far, device_id_type=MESH)

    asks = (1 - late) * crossing

    w_recv[f] = w_send[f]
    for copy in cols_in:
        copy.wait_recv()
    for g in range(count_f):
        w_pack[rows * g : rows * (g + 1), :] = w_recv[g, 0:rows, :].astype(F32)
    wall[y, zh, core] = w_pack[...].astype(BF16)

    ring = {}
    reach_y = NY // 2
    hops = ((reach_y, reach_y - 1), (reach_y - 1, reach_y))
    tiles = wall.shape[-1] // 128
    cut = (tiles + 1) // 2 * 128
    lanes = (pl.ds(0, cut), pl.ds(cut, tiles * 128 - cut))

    def at(shift):
        return lax.rem(y + shift + NY, NY)

    def piece(source, j, p):
        return wall.at[source, zs[j], core, :, lanes[p]]

    def pass_on(j, hop, p=None):
        if p is None:
            for p in range(len(hops)):
                pass_on(j, hop, p)
            return
        for way, dev, sign in ((0, right, -1), (1, left, 1)):
            last = hops[p][way]
            if 1 <= hop <= last:
                ring[j, p, way].wait_recv()
            if hop < last:
                ref = piece(at(sign * hop), j, p)
                ring[j, p, way] = send(ref, ref, dev)

    def half_of(j):
        return lax.div(zs[j], 2)

    shared = {}

    def share(j, shift):
        ref = wall.at[at(shift), pl.ds(2 * half_of(j), 2), core]
        shared[j, shift] = send(ref, ref, sibling)

    pass_on(0, 0)
    z_in = {}
    for p in range(len(hops)):
        z_in[1, p] = send(piece(y, 0, p), piece(y, 0, p), z_peers[1])
    for p in range(len(hops)):
        z_in[3, p] = prepare(piece(y, 0, p), piece(y, 0, p), z_peers[3])

    @pl.when(late == 1)
    def _():
        for p in range(len(hops)):
            z_in[3, p].start()


    first_pos = me * tok
    seq_total = tok * count_c
    scale_qk = 1.0 / math.sqrt(HEAD)

    def attend(block):
        start = pl.multiple_of(block * reach, reach)
        part = pl.ds(start, reach)
        shape = (reach, 3 * reach)
        row_id = lax.broadcasted_iota(jnp.int32, shape, 0)
        col_id = lax.broadcasted_iota(jnp.int32, shape, 1)
        key_pos = first_pos + (start - reach) + col_id
        offset = col_id - row_id
        allowed = (
            (offset >= 0) & (offset <= 2 * reach) & (key_pos >= 0) & (key_pos < seq_total)
        )
        for h in range(feat // HEAD):
            cols = slice(h * HEAD, (h + 1) * HEAD)
            qs = q_buf[part, cols]
            ks = kv_buf[0, pl.ds(start, 3 * reach), cols]
            vs = kv_buf[1, pl.ds(start, 3 * reach), cols]
            scores = (
                lax.dot_general(qs, ks, (((1,), (1,)), ((), ())), preferred_element_type=F32)
                * scale_qk
            )
            masked = jnp.where(allowed, scores, -jnp.inf)
            row_max = jnp.max(masked, axis=1, keepdims=True)
            terms = jnp.exp(masked - row_max)
            probs = (terms / jnp.sum(terms, axis=1, keepdims=True)).astype(BF16)
            attended = jnp.dot(probs, vs, preferred_element_type=F32).astype(BF16)
            resid = r_buf[part, cols].astype(F32)
            gate = gate_buf[cols].reshape(1, HEAD)
            xg[f, part, cols] = (resid + gate * attended.astype(F32)).astype(BF16)
        mine = xg.at[f, part]
        return [send(mine, mine, dev) for dev in [(me, beside)] + x_peers]

    def part_of(order):
        return pl.ds(pl.multiple_of(((1 - core) if order == 0 else core) * reach, reach), reach)

    def relay(order):
        x_in[order].pop(0).wait_recv()
        theirs = xg.at[beside, part_of(order)]
        x_in[order] += [send(theirs, theirs, dev) for dev in x_peers]

    def normalise(order):
        for copy in x_in[order]:
            copy.wait_recv()
        part = part_of(order)
        total = jnp.zeros((reach, feat), F32)
        for g in range(count_f):
            total += xg[g, part, :].astype(F32)
        mean = jnp.sum(total, axis=1, keepdims=True) / d_model
        total = jnp.zeros((reach, feat), F32)
        for g in range(count_f):
            centered = xg[g, part, :].astype(F32) - mean
            total += centered * centered
        inv = lax.rsqrt(jnp.sum(total, axis=1, keepdims=True) / d_model + 1e-06)
        for g in range(count_f):
            centered = xg[g, part, :].astype(F32) - mean
            xn[g, part, :] = (centered * inv * vecs[g, 0:1, :] + vecs[g, 1:2, :]).astype(BF16)

    def multiply(shift, first=False):
        shared[1, shift].wait_recv()
        shared[3, shift].wait_recv()
        source = at(shift)
        weights = wall[source].reshape(NZ * NC * rows * count_f, wall.shape[-1])
        part = jnp.dot(xn[source], weights, preferred_element_type=F32)
        if first:
            acc[...] = part
        else:
            acc[...] += part

    @pl.when(asks == 0)
    def _():
        far_halo.start()

    near_halo.wait_recv()
    x_in = [attend(1 - core)]
    pass_on(0, 1)

    @pl.when(late == 0)
    def _():
        pl.semaphore_wait(ready_sem.at[0], 1)
        for p in range(len(hops)):
            z_in[3, p].start()

    @pl.when(asks == 1)
    def _():
        pl.semaphore_wait(ready_sem.at[1], 1)
        far_halo.start()

    for p in range(len(hops)):
        z_in[1, p].wait_recv()
        pass_on(1, 0, p)
    pass_on(0, 2)
    relay(0)
    vecs_in = [send(vecs.at[f], vecs.at[f], dev) for dev in f_peers]
    share(1, 0)
    pass_on(1, 1)
    for p in range(len(hops)):
        z_in[3, p].wait_recv()
        z_in[2, p] = send(piece(y, 3, p), piece(y, 3, p), z_peers[1])
        pass_on(3, 0, p)
    pass_on(0, 3)
    far_halo.wait_recv()
    x_in.append(attend(core))
    store_res = pltpu.make_async_copy(xg.at[f], res_hbm, local_sem.at[len(loads)])
    store_res.start()
    share(1, -1)
    share(1, 1)
    pass_on(1, 2)
    share(1, -2)
    share(1, 2)
    for p in range(len(hops)):
        z_in[2, p].wait_recv()
        pass_on(2, 0, p)
    share(3, 0)
    pass_on(0, 4)
    pass_on(3, 1)
    relay(1)
    pass_on(1, 3)
    share(1, -3)
    share(1, 3)
    pass_on(2, 1)
    share(3, -1)
    share(3, 1)
    pass_on(1, 4)
    share(1, reach_y)
    pass_on(3, 2)
    for copy in vecs_in:
        copy.wait_recv()
    normalise(0)
    pass_on(2, 2)
    share(3, -2)
    share(3, 2)
    pass_on(3, 3)
    pass_on(2, 3)
    share(3, -3)
    share(3, 3)
    normalise(1)
    multiply(0, first=True)
    multiply(-1)
    multiply(1)
    multiply(-2)
    multiply(2)
    multiply(-3)
    multiply(3)
    pass_on(3, 4)
    pass_on(2, 4)
    share(3, reach_y)
    multiply(reach_y)

    pre = acc[:, 0:wide] + bias_buf[...].reshape(1, wide)
    hid_buf[...] = jax.nn.gelu(pre, approximate=True).astype(BF16)
    store_hid = pltpu.make_async_copy(hid_buf, hid_hbm, local_sem.at[len(loads) + 1])
    store_hid.start()
    for copy in started:
        copy.wait_send()
    store_res.wait()
    store_hid.wait()


def shards(query_act, key_act, value_act, resid_in, gate_vec, mod_scale, mod_shift, w_up, bias_up):
    tok, feat = query_act.shape
    count_f = lax.axis_size("fsdp")
    wide = bias_up.shape[0]
    padded = -(-wide // 128) * 128
    rows = w_up.shape[0]
    row_pad = -(-rows // 8) * 8
    sends = 4 * (count_f - 1) + 2 + 2 * (NZ - 1) + 2 * NZ * (NY - 1) + 2 * NY
    anywhere = pl.BlockSpec(memory_space=pl.ANY)
    return pl.pallas_call(
        functools.partial(kernel, count_f),
        out_shape=(
            jax.ShapeDtypeStruct((tok, feat), BF16),
            jax.ShapeDtypeStruct((tok, wide), BF16),
        ),
        in_specs=[anywhere] * 9,
        out_specs=(anywhere, anywhere),
        scratch_shapes=[
            pltpu.VMEM((tok, feat), BF16),
            pltpu.VMEM((2, 2 * tok, feat), BF16),
            pltpu.VMEM((tok, feat), BF16),
            pltpu.VMEM((feat,), F32),
            pltpu.VMEM((feat,), F32),
            pltpu.VMEM((feat,), F32),
            pltpu.VMEM((rows, w_up.shape[1]), BF16),
            pltpu.VMEM((wide,), F32),
            pltpu.VMEM((count_f, row_pad, padded), BF16),
            pltpu.VMEM((count_f, row_pad, padded), BF16),
            pltpu.VMEM((rows * count_f, padded), F32),
            pltpu.VMEM((NY, NZ, NC, rows * count_f, padded), BF16),
            pltpu.VMEM((count_f, tok, feat), BF16),
            pltpu.VMEM((count_f, tok, feat), BF16),
            pltpu.VMEM((count_f, 2, feat), F32),
            pltpu.VMEM((tok, padded), F32),
            pltpu.VMEM((tok, wide), BF16),
            pltpu.SemaphoreType.DMA((11,)),
            pltpu.SemaphoreType.DMA((sends,)),
            pltpu.SemaphoreType.DMA((sends,)),
            pltpu.SemaphoreType.REGULAR((2,)),
        ],
        compiler_params=pltpu.CompilerParams(
            collective_id=0, has_side_effects=True, vmem_limit_bytes=48 * 1024 * 1024
        ),
    )(
        pltpu.with_memory_space_constraint(query_act, pltpu.HBM),
        pltpu.with_memory_space_constraint(key_act, pltpu.HBM),
        pltpu.with_memory_space_constraint(value_act, pltpu.HBM),
        pltpu.with_memory_space_constraint(resid_in, pltpu.HBM),
        pltpu.with_memory_space_constraint(gate_vec, pltpu.HBM),
        pltpu.with_memory_space_constraint(mod_scale, pltpu.HBM),
        pltpu.with_memory_space_constraint(mod_shift, pltpu.HBM),
        pltpu.with_memory_space_constraint(w_up, pltpu.HBM),
        pltpu.with_memory_space_constraint(bias_up, pltpu.HBM),
    )


def solution(mesh):
    placed = (
        P("ctx", "fsdp"),
        P("ctx", "fsdp"),
        P("ctx", "fsdp"),
        P("ctx", "fsdp"),
        P("fsdp"),
        P("fsdp"),
        P("fsdp"),
        P(("ctx", "fsdp"), None),
        P("fsdp"),
    )
    return jax.shard_map(
        shards,
        mesh=mesh,
        in_specs=placed,
        out_specs=(P("ctx", "fsdp"), P("ctx", "fsdp")),
        check_vma=False,
    )
```
